32 devices in a mesh: groups: 2 (over y), blk: 4 (over z), sub: 2 (over x), pair: 2 (over core).
Axes of the slice: x: 2, y: 2, z: 4, core: 2. Of those that a mesh axis runs over, the one named last changes fastest.
Arguments:
- resid: bfloat16 [512, 8192], P(('groups', 'blk'), ('sub', 'pair')), parts along dimension 0, may hold values from -6 to 6
- context: bfloat16 [512, 8192], P('groups', 'blk'), parts along dimension 0, may hold values from -6 to 6
- w_out: bfloat16 [8192, 8192], P('blk', ('sub', 'pair')), may hold values from -0.0625 to 0.0625
- w_in: bfloat16 [8192, 14336], P(('sub', 'pair'), 'blk'), may hold values from -0.0625 to 0.0625
- w_down: bfloat16 [14336, 8192], P('blk', ('sub', 'pair')), may hold values from -0.046875 to 0.046875
- scales: float32 [3], replicated, may hold values from 0.5 to 2
Outputs:
- result: bfloat16 [512, 8192], P(('groups', 'blk'), ('sub', 'pair')), parts along dimension 0
The draws below stay inside these ranges and needn't reach their ends.
There are 2 independent parts, one for each index of `groups`. The reference program is written for one: setup_inputs(seed, part) draws one part's arguments, and reference() takes and returns one part's arrays. A program takes and returns all parts, laid end to end along the dimension named above; an argument that names none is the same for every part. Nothing has to cross between parts.
All inputs are finite; a program needn't handle non-finite values.
Results may differ from the reference program's by a relative error of at most 0.025.
Values may be sent and summed in bfloat16 or wider, within the bound.
A program may use at most 128 MiB of HBM per device.

```python
import math
import jax
import jax.numpy as jnp
from jax import lax

D = 8192
HID = 14336
TOKENS = 256
N_BLK = 4
N_SUB = 2
N_PAIR = 2


def steps_of(own_key, extent, shards, smallest, largest):
    factor_of = 1.0
    for dim, blocks in shards:
        heights = jax.random.uniform(jax.random.fold_in(jax.random.fold_in(own_key, 6), dim), (blocks,), jnp.float32, smallest / len(shards), largest / len(shards))
        factor_of = factor_of * jnp.repeat(jnp.exp(heights), extent[dim] // blocks).reshape((-1,) + (1,) * (len(extent) - 1 - dim))
    return factor_of


def scatter_about(stream_key, dims, scale, reach, cuts=(), kind=jnp.bfloat16):
    gain = steps_of(stream_key, dims, cuts, -0.22, 0.18) if cuts else 1.0
    values = jax.random.normal(stream_key, dims, jnp.float32) * scale * gain
    return jnp.minimum(jnp.maximum(values, -reach), reach).astype(kind)


def setup_inputs(seed: int = 0, part: int = 0) -> dict:
    arg_keys = jax.random.split(jax.random.key(seed), 7)
    own_keys = jax.random.split(jax.random.fold_in(arg_keys[6], part), 7)
    return {
        "resid": scatter_about(own_keys[0], (TOKENS, D), 1.0, 6.0, ((0, 4), (1, 4))),
        "context": scatter_about(own_keys[1], (TOKENS, D), 1.0, 6.0, ((1, 4),)),
        "w_out": scatter_about(arg_keys[2], (D, D), D ** -0.5, 0.0625, ((0, 4), (1, 4))),
        "w_in": scatter_about(arg_keys[3], (D, HID), D ** -0.5, 0.0625, ((0, 4), (1, 4))),
        "w_down": scatter_about(arg_keys[4], (HID, D), HID ** -0.5, 0.046875, ((0, 4), (1, 4))),
        "scales": jnp.clip(jnp.exp(jax.random.uniform(arg_keys[5], (3,), jnp.float32, math.log(0.5), math.log(2.0))), 0.5, 2.0),
    }


def block_sum(left, right, parts):
    width = left.shape[1] // parts
    total = jnp.zeros((left.shape[0], right.shape[1]), jnp.float32)
    for index in range(parts):
        term = jnp.dot(left[:, index * width:(index + 1) * width], right[index * width:(index + 1) * width], preferred_element_type=jnp.float32)
        rounded = lax.optimization_barrier(term.astype(jnp.bfloat16))
        total = total + rounded.astype(jnp.float32)
    return total


def reference(resid, context, w_out, w_in, w_down, scales):
    attn = block_sum(context, w_out, N_BLK)
    mixed = (resid.astype(jnp.float32) + scales[0] * attn).astype(jnp.bfloat16)
    pre = block_sum(mixed, w_in, N_SUB * N_PAIR)
    hidden = jax.nn.gelu(scales[1] * pre, approximate=False).astype(jnp.bfloat16)
    mlp = block_sum(hidden, w_down, N_BLK)
    return (mixed.astype(jnp.float32) + scales[2] * mlp).astype(jnp.bfloat16)
```

```python
import functools

import jax
import jax.numpy as jnp
from jax import lax
from jax.experimental import pallas as pl
from jax.experimental.pallas import tpu as pltpu
from jax.sharding import PartitionSpec as P

F32 = jnp.float32
BF16 = jnp.bfloat16
MESH = pl.DeviceIdType.MESH
CHUNKS = 4
TILES = 4
SUBS = 4
ACT = 3
GAP = 1
SKEW = 3
DOWN = 8


def local(resid, context, w_out, w_in, w_down, scales):
    picked = context
    attn = lax.psum_scatter(
        jnp.dot(picked, w_out, preferred_element_type=jnp.float32).astype(jnp.bfloat16),
        "blk",
        scatter_dimension=0,
        tiled=True,
    ).astype(jnp.float32)
    mixed = (resid.astype(jnp.float32) + scales[0] * attn).astype(jnp.bfloat16)
    pre_terms = jnp.dot(
        lax.all_gather(mixed, "blk", axis=0, tiled=True), w_in, preferred_element_type=jnp.float32
    )
    pre_part = lax.psum_scatter(
        pre_terms.astype(jnp.bfloat16), ("sub", "pair"), scatter_dimension=0, tiled=True
    ).astype(jnp.float32)
    hidden_part = jax.nn.gelu(scales[1] * pre_part, approximate=False).astype(jnp.bfloat16)
    hidden = lax.all_gather(hidden_part, ("sub", "pair"), axis=0, tiled=True)
    picked = hidden
    mlp = lax.psum_scatter(
        jnp.dot(picked, w_down, preferred_element_type=jnp.float32).astype(jnp.bfloat16),
        "blk",
        scatter_dimension=0,
        tiled=True,
    ).astype(jnp.float32)
    return (mixed.astype(jnp.float32) + scales[2] * mlp).astype(jnp.bfloat16)


def gelu(v):
    return v * (1.0 + lax.erf(v * (0.5**0.5))) * 0.5


def kernel(
    nb, scales, resid, ctx, wo, wi, wd, out,
    ctxv, residv, wov, wiv, wdv, part, rsend, rrecv, lsend, lrecv, mixed, pre,
    psend, precv, xsend, xrecv, hid, macc, mpart, mrecv,
    ctx_sem, res_sem, wo_sem, wi_sem, wd_sem,
    rss, rrs, lss, lrs, pss, prs, xss, xrs, hss, hrs, mss, mrs,
):
    z, x, p = lax.axis_index("blk"), lax.axis_index("sub"), lax.axis_index("pair")
    last = nb - 1
    tb = residv.shape[0]
    rb = tb // CHUNKS
    rows = rb * nb
    dj = wov.shape[2]
    hq = pre.shape[3]
    rs = rows // SUBS
    n = CHUNKS * TILES

    def ctx_copy(h, b):
        return pltpu.make_async_copy(
            ctx.at[pl.ds(b * tb + h * rb, rb)], ctxv.at[pl.ds(h * rows + b * rb, rb)], ctx_sem.at[h * nb + b]
        )

    def wo_copy(j):
        return pltpu.make_async_copy(wo.at[:, pl.ds(j * dj, dj)], wov.at[j], wo_sem.at[j])

    def wi_copy(j, q):
        return pltpu.make_async_copy(
            wi.at[pl.ds(j * dj, dj), pl.ds(q * hq, hq)], wiv.at[j, q], wi_sem.at[j * 2 + q]
        )

    def wd_copy(j):
        return pltpu.make_async_copy(wd.at[:, pl.ds(pl.multiple_of(j * dj, dj), dj)], wdv.at[j], wd_sem.at[j])

    res_copy = pltpu.make_async_copy(resid, residv, res_sem)

    def remote(src, dst, ss, rsm, dev):
        return pltpu.make_async_remote_copy(
            src_ref=src, dst_ref=dst, send_sem=ss, recv_sem=rsm, device_id=dev, device_id_type=MESH
        )

    def rcopy(c):
        return remote(rsend.at[c], rrecv.at[c], rss.at[c], rrs.at[c], {"blk": lax.rem(z + 1, nb)})

    def lcopy(c):
        return remote(lsend.at[c], lrecv.at[c], lss.at[c], lrs.at[c], {"blk": lax.rem(z + last, nb)})

    def pcopy(h):
        return remote(psend.at[h], precv.at[h], pss.at[h], prs.at[h], {"pair": 1 - p})

    def piece(i):
        return pl.ds(pl.multiple_of(i * rs, rs), rs)

    def xcopy(h, i):
        return remote(
            xsend.at[h, piece(i)], xrecv.at[h, piece(i)], xss.at[h * SUBS + i], xrs.at[h * SUBS + i], {"sub": 1 - x}
        )

    def hcopy(h, i, q):
        return remote(
            hid.at[h, q, piece(i)], hid.at[h, q, piece(i)], hss.at[h * SUBS + i], hrs.at[h * SUBS + i], {"pair": 1 - p}
        )

    def mcopy(h, j, d):
        to = lax.rem(z + d, nb)
        k = (h * TILES + j) * last + d - 1
        return remote(mpart.at[h, j, to], mrecv.at[h, j, d - 1], mss.at[k], mrs.at[k], {"blk": to})

    for h in range(CHUNKS):
        for b in range(nb):
            ctx_copy(h, b).start()
    for j in range(TILES):
        wo_copy(j).start()
    res_copy.start()

    barrier = pltpu.get_barrier_semaphore()
    for d in range(1, nb):
        pl.semaphore_signal(barrier, inc=1, device_id={"blk": lax.rem(z + d, nb)}, device_id_type=MESH)
    pl.semaphore_signal(barrier, inc=1, device_id={"sub": 1 - x}, device_id_type=MESH)
    pl.semaphore_signal(barrier, inc=1, device_id={"pair": 1 - p}, device_id_type=MESH)

    pre[...] = jnp.zeros_like(pre)

    @pl.when(z == 0)
    def _():
        rrecv[...] = jnp.zeros_like(rrecv)

    @pl.when(z == last)
    def _():
        lrecv[...] = jnp.zeros_like(lrecv)

    for h in range(CHUNKS):
        for b in range(nb):
            ctx_copy(h, b).wait()
    res_copy.wait()

    mine = pl.ds(pl.multiple_of(z * rb, rb), rb)
    far = jnp.maximum(z, last - z)

    def lead(c):
        @pl.when(z == 0)
        def _():
            rsend[c] = part[c].astype(BF16)
            rcopy(c).start()

        @pl.when(z == last)
        def _():
            lsend[c] = part[c].astype(BF16)
            lcopy(c).start()

    for j in range(TILES):
        wo_copy(j).wait()
        for q in range(2):
            wi_copy(j, q).start()
        acc = scales[0] * jnp.dot(ctxv[...], wov[j], preferred_element_type=F32)
        for h in range(CHUNKS):
            c = h * TILES + j
            part[c] = acc[h * rows:(h + 1) * rows]
            part[c, mine] = part[c, mine] + residv[h * rb:(h + 1) * rb, j * dj:(j + 1) * dj].astype(F32)
        if j == 0:
            pl.semaphore_wait(barrier, nb + 1)
        lead(j)

    def leads(c, carry):
        lead(c)
        return carry

    lax.fori_loop(TILES, n, leads, 0)

    def cross(h):
        pcopy(h).wait_recv()
        total = pre[h, p] + precv[h].astype(F32)
        pre[h, p] = total
        xsend[h] = total.astype(BF16)
        for i in range(SUBS):
            xcopy(h, i).start()

    def activate(h, i):
        xcopy(h, i).wait_recv()
        v = pre[h, p, piece(i)] + xrecv[h, piece(i)].astype(F32)
        hid[h, p, piece(i)] = gelu(scales[1] * v).astype(BF16)
        hcopy(h, i, p).start()

    def down(h, j):
        @pl.when(j == 0)
        def _():
            for i in range(SUBS):
                hcopy(h, i, 1 - p).wait_recv()

        @pl.when(h == 0)
        def _():
            wd_copy(j).wait()

        total = jnp.dot(hid[h, 0], wdv[j, :hq], preferred_element_type=F32)
        total += jnp.dot(hid[h, 1], wdv[j, hq:], preferred_element_type=F32)
        total = total.reshape(nb, rb, dj)
        macc[h, j] = total
        mpart[h, j] = total.astype(BF16)
        for d in range(1, nb):
            mcopy(h, j, d).start()

    def step(s, carry):
        cr, cl, cm = s - SKEW * (z - 1), s - SKEW * (last - z - 1), s - SKEW * (far - 1)

        @pl.when(s < TILES)
        def _():
            wd_copy(s).start()

        right = (cr >= 0) & (cr < n) & (z > 0)
        left = (cl >= 0) & (cl < n) & (z < last)

        @pl.when(right)
        def _():
            rcopy(cr).wait_recv()

            @pl.when(z < last)
            def _():
                rsend[cr] = (part[cr] + rrecv[cr].astype(F32)).astype(BF16)
                rcopy(cr).start()

        @pl.when(left)
        def _():
            lcopy(cl).wait_recv()

            @pl.when(z > 0)
            def _():
                lsend[cl] = (part[cl] + lrecv[cl].astype(F32)).astype(BF16)
                lcopy(cl).start()

        @pl.when((cm >= TILES) & (cm <= n) & (lax.rem(jnp.maximum(cm, 0), TILES) == 0))
        def _():
            cross(cm // TILES - 1)

        @pl.when((cm >= 0) & (cm < n))
        def _():
            h, j = cm // TILES, lax.rem(cm, TILES)
            mixed[cm] = (part[cm] + rrecv[cm].astype(F32) + lrecv[cm].astype(F32)).astype(BF16)

            @pl.when(cm < TILES)
            def _():
                for q in range(2):
                    wi_copy(j, q).wait()

            pre[h, 1 - p] += jnp.dot(mixed[cm], wiv[j, 1 - p], preferred_element_type=F32)

            @pl.when(j == TILES - 1)
            def _():
                psend[h] = pre[h, 1 - p].astype(BF16)
                pcopy(h).start()

            pre[h, p] += jnp.dot(mixed[cm], wiv[j, p], preferred_element_type=F32)

        for i in range(SUBS):
            ca = jnp.maximum(cm - TILES - ACT - GAP * i, -1)

            @pl.when((ca >= 0) & (ca < n) & (lax.rem(jnp.maximum(ca, 0), TILES) == 0))
            def _():
                activate(ca // TILES, i)

        cd = jnp.maximum(cm - TILES - DOWN, -1)

        @pl.when((cd >= 0) & (cd < n))
        def _():
            down(cd // TILES, lax.rem(cd, TILES))

        return carry

    lax.fori_loop(0, n + SKEW * (last - 1) + TILES + DOWN, step, 0)

    for h in range(CHUNKS):
        for j in range(TILES):
            total = macc[h, j, z]
            for d in range(1, nb):
                mcopy(h, j, d).wait_recv()
                total += mrecv[h, j, d - 1].astype(F32)
            base = mixed[h * TILES + j, mine].astype(F32)
            out[h * rb:(h + 1) * rb, j * dj:(j + 1) * dj] = (base + scales[2] * total).astype(BF16)

    @pl.when(z < last)
    def _():
        for c in range(n):
            rcopy(c).wait_send()

    @pl.when(z > 0)
    def _():
        for c in range(n):
            lcopy(c).wait_send()

    for h in range(CHUNKS):
        pcopy(h).wait_send()
        for i in range(SUBS):
            xcopy(h, i).wait_send()
            hcopy(h, i, p).wait_send()
        for j in range(TILES):
            for d in range(1, nb):
                mcopy(h, j, d).wait_send()


def fused(nb, resid, context, w_out, w_in, w_down, scales):
    tb, d = resid.shape
    t, k = context.shape
    hidden = w_in.shape[1]
    rows, dj, hq, rb = t // CHUNKS, d // TILES, hidden // 2, tb // CHUNKS
    n, last = CHUNKS * TILES, nb - 1
    any_spec = pl.BlockSpec(memory_space=pl.ANY)
    dma = pltpu.SemaphoreType.DMA
    return pl.pallas_call(
        functools.partial(kernel, nb),
        out_shape=jax.ShapeDtypeStruct((tb, d), BF16),
        in_specs=[pl.BlockSpec(memory_space=pltpu.SMEM)] + [any_spec] * 5,
        out_specs=pl.BlockSpec(memory_space=pltpu.VMEM),
        scratch_shapes=[
            pltpu.VMEM((t, k), BF16),
            pltpu.VMEM((tb, d), BF16),
            pltpu.VMEM((TILES, k, dj), BF16),
            pltpu.VMEM((TILES, 2, dj, hq), BF16),
            pltpu.VMEM((TILES, hidden, dj), BF16),
            pltpu.VMEM((n, rows, dj), F32),
            pltpu.VMEM((n, rows, dj), BF16),
            pltpu.VMEM((n, rows, dj), BF16),
            pltpu.VMEM((n, rows, dj), BF16),
            pltpu.VMEM((n, rows, dj), BF16),
            pltpu.VMEM((n, rows, dj), BF16),
            pltpu.VMEM((CHUNKS, 2, rows, hq), F32),
            pltpu.VMEM((CHUNKS, rows, hq), BF16),
            pltpu.VMEM((CHUNKS, rows, hq), BF16),
            pltpu.VMEM((CHUNKS, rows, hq), BF16),
            pltpu.VMEM((CHUNKS, rows, hq), BF16),
            pltpu.VMEM((CHUNKS, 2, rows, hq), BF16),
            pltpu.VMEM((CHUNKS, TILES, nb, rb, dj), F32),
            pltpu.VMEM((CHUNKS, TILES, nb, rb, dj), BF16),
            pltpu.VMEM((CHUNKS, TILES, last, rb, dj), BF16),
            dma((CHUNKS * nb,)), dma, dma((TILES,)), dma((TILES * 2,)), dma((TILES,)),
            dma((n,)), dma((n,)), dma((n,)), dma((n,)),
            dma((CHUNKS,)), dma((CHUNKS,)),
            dma((CHUNKS * SUBS,)), dma((CHUNKS * SUBS,)),
            dma((CHUNKS * SUBS,)), dma((CHUNKS * SUBS,)),
            dma((n * last,)), dma((n * last,)),
        ],
        compiler_params=pltpu.CompilerParams(
            collective_id=0, has_side_effects=True, vmem_limit_bytes=67043328
        ),
    )(scales, resid, context, w_out, w_in, w_down)


def solution(mesh):
    in_specs = (
        P(("groups", "blk"), ("sub", "pair")),
        P("groups", "blk"),
        P("blk", ("sub", "pair")),
        P(("sub", "pair"), "blk"),
        P("blk", ("sub", "pair")),
        P(),
    )
    out_specs = P(("groups", "blk"), ("sub", "pair"))
    nb = mesh.shape["blk"]
    if mesh.shape["sub"] == 2 and mesh.shape["pair"] == 2 and nb > 1:
        body = functools.partial(fused, nb)
    else:
        body = local
    return jax.shard_map(body, mesh=mesh, in_specs=in_specs, out_specs=out_specs, check_vma=False)
```

```python
import functools

import jax
import jax.numpy as jnp
from jax import lax
from jax.experimental import pallas as pl
from jax.experimental.pallas import tpu as pltpu
from jax.sharding import PartitionSpec as P

F32 = jnp.float32
BF16 = jnp.bfloat16
MESH = pl.DeviceIdType.MESH
CHUNKS = 4
TILES = 4
SUBS = 2
ACT = 5
GAP = 2
SKEW = 3
DOWN = 9


def local(resid, context, w_out, w_in, w_down, scales):
    picked = context
    attn = lax.psum_scatter(
        jnp.dot(picked, w_out, preferred_element_type=jnp.float32).astype(jnp.bfloat16),
        "blk",
        scatter_dimension=0,
        tiled=True,
    ).astype(jnp.float32)
    mixed = (resid.astype(jnp.float32) + scales[0] * attn).astype(jnp.bfloat16)
    pre_terms = jnp.dot(
        lax.all_gather(mixed, "blk", axis=0, tiled=True), w_in, preferred_element_type=jnp.float32
    )
    pre_part = lax.psum_scatter(
        pre_terms.astype(jnp.bfloat16), ("sub", "pair"), scatter_dimension=0, tiled=True
    ).astype(jnp.float32)
    hidden_part = jax.nn.gelu(scales[1] * pre_part, approximate=False).astype(jnp.bfloat16)
    hidden = lax.all_gather(hidden_part, ("sub", "pair"), axis=0, tiled=True)
    picked = hidden
    mlp = lax.psum_scatter(
        jnp.dot(picked, w_down, preferred_element_type=jnp.float32).astype(jnp.bfloat16),
        "blk",
        scatter_dimension=0,
        tiled=True,
    ).astype(jnp.float32)
    return (mixed.astype(jnp.float32) + scales[2] * mlp).astype(jnp.bfloat16)


def gelu(v):
    return v * (1.0 + lax.erf(v * (0.5**0.5))) * 0.5


def kernel(
    nb, scales, resid, ctx, wo, wi, wd, out,
    ctxv, residv, wov, wiv, wdv, part, rsend, rrecv, lsend, lrecv, mixed, pre,
    psend, precv, xsend, xrecv, hid, macc, mpart, mrecv,
    ctx_sem, res_sem, wo_sem, wi_sem, wd_sem,
    rss, rrs, lss, lrs, pss, prs, xss, xrs, hss, hrs, mss, mrs,
):
    z, x, p = lax.axis_index("blk"), lax.axis_index("sub"), lax.axis_index("pair")
    last = nb - 1
    tb = residv.shape[0]
    rb = tb // CHUNKS
    rows = rb * nb
    dj = wov.shape[2]
    hq = pre.shape[3]
    rs = rows // SUBS
    n = CHUNKS * TILES

    def ctx_copy(h):
        return pltpu.make_async_copy(ctx.at[:, h], ctxv.at[h], ctx_sem.at[h])

    def wo_copy(j):
        return pltpu.make_async_copy(wo.at[:, pl.ds(j * dj, dj)], wov.at[j], wo_sem.at[j])

    def wi_copy(j, q):
        return pltpu.make_async_copy(
            wi.at[pl.ds(j * dj, dj), pl.ds(q * hq, hq)], wiv.at[j, q], wi_sem.at[j * 2 + q]
        )

    def wd_copy(j):
        return pltpu.make_async_copy(wd.at[:, pl.ds(pl.multiple_of(j * dj, dj), dj)], wdv.at[j], wd_sem.at[j])

    res_copy = pltpu.make_async_copy(resid, residv, res_sem)

    def remote(src, dst, ss, rsm, dev):
        return pltpu.make_async_remote_copy(
            src_ref=src, dst_ref=dst, send_sem=ss, recv_sem=rsm, device_id=dev, device_id_type=MESH
        )

    def rcopy(c):
        return remote(rsend.at[c], rrecv.at[c], rss.at[c], rrs.at[c], {"blk": lax.rem(z + 1, nb)})

    def lcopy(c):
        return remote(lsend.at[c], lrecv.at[c], lss.at[c], lrs.at[c], {"blk": lax.rem(z + last, nb)})

    def pcopy(h):
        return remote(psend.at[h], precv.at[h], pss.at[h], prs.at[h], {"pair": 1 - p})

    def piece(i):
        return pl.ds(pl.multiple_of(i * rs, rs), rs)

    def xcopy(h, i):
        return remote(
            xsend.at[h, piece(i)], xrecv.at[h, piece(i)], xss.at[h * SUBS + i], xrs.at[h * SUBS + i], {"sub": 1 - x}
        )

    def hcopy(h, i, q):
        return remote(
            hid.at[h, q, piece(i)], hid.at[h, q, piece(i)], hss.at[h * SUBS + i], hrs.at[h * SUBS + i], {"pair": 1 - p}
        )

    def mcopy(h, j, d):
        to = lax.rem(z + d, nb)
        k = (h * TILES + j) * last + d - 1
        return remote(mpart.at[h, j, to], mrecv.at[h, j, d - 1], mss.at[k], mrs.at[k], {"blk": to})

    barrier = pltpu.get_barrier_semaphore()
    for d in (1, -1):
        @pl.when((z + d >= 0) & (z + d < nb))
        def _():
            pl.semaphore_signal(barrier, inc=1, device_id={"blk": z + d}, device_id_type=MESH)
    pl.semaphore_signal(barrier, inc=1, device_id={"sub": 1 - x}, device_id_type=MESH)
    pl.semaphore_signal(barrier, inc=1, device_id={"pair": 1 - p}, device_id_type=MESH)

    wo_copy(0).start()
    for h in range(CHUNKS):
        ctx_copy(h).start()
    for j in range(1, TILES):
        wo_copy(j).start()
    res_copy.start()

    pre[...] = jnp.zeros_like(pre)

    @pl.when(z == 0)
    def _():
        rrecv[...] = jnp.zeros_like(rrecv)

    @pl.when(z == last)
    def _():
        lrecv[...] = jnp.zeros_like(lrecv)

    for h in range(CHUNKS):
        ctx_copy(h).wait()
    res_copy.wait()

    mine = pl.ds(pl.multiple_of(z * rb, rb), rb)
    far = jnp.maximum(z, last - z)

    def lead(c):
        @pl.when(z == 0)
        def _():
            rsend[c] = part[c].astype(BF16)
            rcopy(c).start()

        @pl.when(z == last)
        def _():
            lsend[c] = part[c].astype(BF16)
            lcopy(c).start()

    for j in range(TILES):
        wo_copy(j).wait()
        for q in range(2):
            wi_copy(j, q).start()
        acc = scales[0] * jnp.dot(ctxv[...].reshape(CHUNKS * rows, -1), wov[j], preferred_element_type=F32)
        for h in range(CHUNKS):
            c = h * TILES + j
            part[c] = acc[h * rows:(h + 1) * rows]
            part[c, mine] = part[c, mine] + residv[h * rb:(h + 1) * rb, j * dj:(j + 1) * dj].astype(F32)
        if j == 0:
            pl.semaphore_wait(barrier, jnp.where((z > 0) & (z < last), 4, 3))
        lead(j)

    def leads(c, carry):
        lead(c)
        return carry

    lax.fori_loop(TILES, n, leads, 0)

    def cross(h):
        pcopy(h).wait_recv()
        total = pre[h, p] + precv[h].astype(F32)
        pre[h, p] = total
        xsend[h] = total.astype(BF16)
        for i in range(SUBS):
            xcopy(h, i).start()

    def activate(h, i):
        xcopy(h, i).wait_recv()
        v = pre[h, p, piece(i)] + xrecv[h, piece(i)].astype(F32)
        hid[h, p, piece(i)] = gelu(scales[1] * v).astype(BF16)
        hcopy(h, i, p).start()

    def down(h, j):
        @pl.when(j == 0)
        def _():
            for i in range(SUBS):
                hcopy(h, i, 1 - p).wait_recv()

        @pl.when(h == 0)
        def _():
            wd_copy(j).wait()

        total = jnp.dot(hid[h, 0], wdv[j, :hq], preferred_element_type=F32)
        total += jnp.dot(hid[h, 1], wdv[j, hq:], preferred_element_type=F32)
        total = total.reshape(nb, rb, dj)
        macc[h, j] = total
        mpart[h, j] = total.astype(BF16)
        for d in range(1, nb):
            mcopy(h, j, d).start()

    def step(s, carry):
        cr, cl, cm = s - SKEW * (z - 1), s - SKEW * (last - z - 1), s - SKEW * (far - 1)

        @pl.when(s < TILES)
        def _():
            wd_copy(s).start()

        right = (cr >= 0) & (cr < n) & (z > 0)
        left = (cl >= 0) & (cl < n) & (z < last)

        @pl.when(right)
        def _():
            rcopy(cr).wait_recv()

            @pl.when(z < last)
            def _():
                rsend[cr] = (part[cr] + rrecv[cr].astype(F32)).astype(BF16)
                rcopy(cr).start()

        @pl.when(left)
        def _():
            lcopy(cl).wait_recv()

            @pl.when(z > 0)
            def _():
                lsend[cl] = (part[cl] + lrecv[cl].astype(F32)).astype(BF16)
                lcopy(cl).start()

        @pl.when((cm >= TILES) & (cm <= n) & (lax.rem(jnp.maximum(cm, 0), TILES) == 0))
        def _():
            cross(cm // TILES - 1)

        @pl.when((cm >= 0) & (cm < n))
        def _():
            h, j = cm // TILES, lax.rem(cm, TILES)
            mixed[cm] = (part[cm] + rrecv[cm].astype(F32) + lrecv[cm].astype(F32)).astype(BF16)

            @pl.when(cm < TILES)
            def _():
                for q in range(2):
                    wi_copy(j, q).wait()

            pre[h, 1 - p] += jnp.dot(mixed[cm], wiv[j, 1 - p], preferred_element_type=F32)

            @pl.when(j == TILES - 1)
            def _():
                psend[h] = pre[h, 1 - p].astype(BF16)
                pcopy(h).start()

            pre[h, p] += jnp.dot(mixed[cm], wiv[j, p], preferred_element_type=F32)

        for i in range(SUBS):
            ca = jnp.maximum(cm - TILES - ACT - GAP * i, -1)

            @pl.when((ca >= 0) & (ca < n) & (lax.rem(jnp.maximum(ca, 0), TILES) == 0))
            def _():
                activate(ca // TILES, i)

        cd = jnp.maximum(cm - TILES - DOWN, -1)

        @pl.when((cd >= 0) & (cd < n))
        def _():
            down(cd // TILES, lax.rem(cd, TILES))

        return carry

    lax.fori_loop(0, n + SKEW * (last - 1) + TILES + DOWN, step, 0)

    def finish(h):
        for j in range(TILES):
            total = macc[h, j, z]
            for d in range(1, nb):
                mcopy(h, j, d).wait_recv()
                total += mrecv[h, j, d - 1].astype(F32)
            base = mixed[h * TILES + j, mine].astype(F32)
            out[h * rb:(h + 1) * rb, j * dj:(j + 1) * dj] = (base + scales[2] * total).astype(BF16)

    def sent(h):
        for j in range(TILES):
            for d in range(1, nb):
                mcopy(h, j, d).wait_send()

    @pl.when(z < last)
    def _():
        for c in range(n):
            rcopy(c).wait_send()

    @pl.when(z > 0)
    def _():
        for c in range(n):
            lcopy(c).wait_send()

    for h in range(CHUNKS):
        pcopy(h).wait_send()
        for i in range(SUBS):
            xcopy(h, i).wait_send()
            hcopy(h, i, p).wait_send()

    for h in range(CHUNKS - 1):
        finish(h)
        sent(h)
    finish(CHUNKS - 1)
    sent(CHUNKS - 1)


def fused(nb, resid, context, w_out, w_in, w_down, scales):
    tb, d = resid.shape
    t, k = context.shape
    hidden = w_in.shape[1]
    rows, dj, hq, rb = t // CHUNKS, d // TILES, hidden // 2, tb // CHUNKS
    n, last = CHUNKS * TILES, nb - 1
    any_spec = pl.BlockSpec(memory_space=pl.ANY)
    dma = pltpu.SemaphoreType.DMA
    return pl.pallas_call(
        functools.partial(kernel, nb),
        out_shape=jax.ShapeDtypeStruct((tb, d), BF16),
        in_specs=[pl.BlockSpec(memory_space=pltpu.SMEM)] + [any_spec] * 5,
        out_specs=pl.BlockSpec(memory_space=pltpu.VMEM),
        scratch_shapes=[
            pltpu.VMEM((CHUNKS, nb, rb, k), BF16),
            pltpu.VMEM((tb, d), BF16),
            pltpu.VMEM((TILES, k, dj), BF16),
            pltpu.VMEM((TILES, 2, dj, hq), BF16),
            pltpu.VMEM((TILES, hidden, dj), BF16),
            pltpu.VMEM((n, rows, dj), F32),
            pltpu.VMEM((n, rows, dj), BF16),
            pltpu.VMEM((n, rows, dj), BF16),
            pltpu.VMEM((n, rows, dj), BF16),
            pltpu.VMEM((n, rows, dj), BF16),
            pltpu.VMEM((n, rows, dj), BF16),
            pltpu.VMEM((CHUNKS, 2, rows, hq), F32),
            pltpu.VMEM((CHUNKS, rows, hq), BF16),
            pltpu.VMEM((CHUNKS, rows, hq), BF16),
            pltpu.VMEM((CHUNKS, rows, hq), BF16),
            pltpu.VMEM((CHUNKS, rows, hq), BF16),
            pltpu.VMEM((CHUNKS, 2, rows, hq), BF16),
            pltpu.VMEM((CHUNKS, TILES, nb, rb, dj), F32),
            pltpu.VMEM((CHUNKS, TILES, nb, rb, dj), BF16),
            pltpu.VMEM((CHUNKS, TILES, last, rb, dj), BF16),
            dma((CHUNKS,)), dma, dma((TILES,)), dma((TILES * 2,)), dma((TILES,)),
            dma((n,)), dma((n,)), dma((n,)), dma((n,)),
            dma((CHUNKS,)), dma((CHUNKS,)),
            dma((CHUNKS * SUBS,)), dma((CHUNKS * SUBS,)),
            dma((CHUNKS * SUBS,)), dma((CHUNKS * SUBS,)),
            dma((n * last,)), dma((n * last,)),
        ],
        compiler_params=pltpu.CompilerParams(
            collective_id=0, has_side_effects=True, vmem_limit_bytes=67043328
        ),
    )(scales, resid, context.reshape(nb, CHUNKS, rb, k), w_out, w_in, w_down)


def solution(mesh):
    in_specs = (
        P(("groups", "blk"), ("sub", "pair")),
        P("groups", "blk"),
        P("blk", ("sub", "pair")),
        P(("sub", "pair"), "blk"),
        P("blk", ("sub", "pair")),
        P(),
    )
    out_specs = P(("groups", "blk"), ("sub", "pair"))
    nb = mesh.shape["blk"]
    if mesh.shape["sub"] == 2 and mesh.shape["pair"] == 2 and nb > 1:
        body = functools.partial(fused, nb)
    else:
        body = local
    return jax.shard_map(body, mesh=mesh, in_specs=in_specs, out_specs=out_specs, check_vma=False)
```

```python
import functools

import jax
import jax.numpy as jnp
from jax import lax
from jax.experimental import pallas as pl
from jax.experimental.pallas import tpu as pltpu
from jax.sharding import PartitionSpec as P

F32 = jnp.float32
BF16 = jnp.bfloat16
MESH = pl.DeviceIdType.MESH
CHUNKS = 4
TILES = 4
SUBS = 1
ACT = 7
GAP = 2
SKEW = 3
DOWN = 9


def local(resid, context, w_out, w_in, w_down, scales):
    picked = context
    attn = lax.psum_scatter(
        jnp.dot(picked, w_out, preferred_element_type=jnp.float32).astype(jnp.bfloat16),
        "blk",
        scatter_dimension=0,
        tiled=True,
    ).astype(jnp.float32)
    mixed = (resid.astype(jnp.float32) + scales[0] * attn).astype(jnp.bfloat16)
    pre_terms = jnp.dot(
        lax.all_gather(mixed, "blk", axis=0, tiled=True), w_in, preferred_element_type=jnp.float32
    )
    pre_part = lax.psum_scatter(
        pre_terms.astype(jnp.bfloat16), ("sub", "pair"), scatter_dimension=0, tiled=True
    ).astype(jnp.float32)
    hidden_part = jax.nn.gelu(scales[1] * pre_part, approximate=False).astype(jnp.bfloat16)
    hidden = lax.all_gather(hidden_part, ("sub", "pair"), axis=0, tiled=True)
    picked = hidden
    mlp = lax.psum_scatter(
        jnp.dot(picked, w_down, preferred_element_type=jnp.float32).astype(jnp.bfloat16),
        "blk",
        scatter_dimension=0,
        tiled=True,
    ).astype(jnp.float32)
    return (mixed.astype(jnp.float32) + scales[2] * mlp).astype(jnp.bfloat16)


def gelu(v):
    return v * (1.0 + lax.erf(v * (0.5**0.5))) * 0.5


def kernel(
    nb, scales, resid, ctx, wo, wi, wd, out,
    outv, ctxv, residv, wov, wiv, wdv, part, rsend, rrecv, lsend, lrecv, mixed, pre,
    psend, precv, xsend, xrecv, hid, macc, mpart, mrecv,
    out_sem, ctx_sem, res_sem, wo_sem, wi_sem, wd_sem,
    rss, rrs, lss, lrs, pss, prs, xss, xrs, hss, hrs, mss, mrs,
):
    z, x, p = lax.axis_index("blk"), lax.axis_index("sub"), lax.axis_index("pair")
    last = nb - 1
    tb = residv.shape[0]
    rb = tb // CHUNKS
    rows = rb * nb
    dj = wov.shape[2]
    hq = pre.shape[3]
    rs = rows // SUBS
    n = CHUNKS * TILES

    def ctx_copy(h):
        return pltpu.make_async_copy(ctx.at[:, h], ctxv.at[h], ctx_sem.at[h])

    def wo_copy(j):
        return pltpu.make_async_copy(wo.at[:, pl.ds(j * dj, dj)], wov.at[j], wo_sem.at[j])

    def wi_copy(j, q):
        return pltpu.make_async_copy(
            wi.at[pl.ds(j * dj, dj), pl.ds(q * hq, hq)], wiv.at[j, q], wi_sem.at[j * 2 + q]
        )

    def wd_copy(j):
        return pltpu.make_async_copy(wd.at[:, pl.ds(pl.multiple_of(j * dj, dj), dj)], wdv.at[j], wd_sem.at[j])

    res_copy = pltpu.make_async_copy(resid, residv, res_sem)

    def remote(src, dst, ss, rsm, dev):
        return pltpu.make_async_remote_copy(
            src_ref=src, dst_ref=dst, send_sem=ss, recv_sem=rsm, device_id=dev, device_id_type=MESH
        )

    def rcopy(c):
        return remote(rsend.at[c], rrecv.at[c], rss.at[c], rrs.at[c], {"blk": lax.rem(z + 1, nb)})

    def lcopy(c):
        return remote(lsend.at[c], lrecv.at[c], lss.at[c], lrs.at[c], {"blk": lax.rem(z + last, nb)})

    def pcopy(h):
        return remote(psend.at[h], precv.at[h], pss.at[h], prs.at[h], {"pair": 1 - p})

    def piece(i):
        return pl.ds(pl.multiple_of(i * rs, rs), rs)

    def xcopy(h, i):
        return remote(
            xsend.at[h, piece(i)], xrecv.at[h, piece(i)], xss.at[h * SUBS + i], xrs.at[h * SUBS + i], {"sub": 1 - x}
        )

    def hcopy(h, i, q):
        return remote(
            hid.at[h, q, piece(i)], hid.at[h, q, piece(i)], hss.at[h * SUBS + i], hrs.at[h * SUBS + i], {"pair": 1 - p}
        )

    def mcopy(h, j, d):
        to = lax.rem(z + d, nb)
        k = (h * TILES + j) * last + d - 1
        return remote(mpart.at[h, j, to], mrecv.at[h, j, d - 1], mss.at[k], mrs.at[k], {"blk": to})

    barrier = pltpu.get_barrier_semaphore()
    for d in (1, -1):
        @pl.when((z + d >= 0) & (z + d < nb))
        def _():
            pl.semaphore_signal(barrier, inc=1, device_id={"blk": z + d}, device_id_type=MESH)
    pl.semaphore_signal(barrier, inc=1, device_id={"sub": 1 - x}, device_id_type=MESH)
    pl.semaphore_signal(barrier, inc=1, device_id={"pair": 1 - p}, device_id_type=MESH)

    wo_copy(0).start()
    for h in range(CHUNKS):
        ctx_copy(h).start()
    for j in range(1, TILES):
        wo_copy(j).start()
    res_copy.start()

    pre[...] = jnp.zeros_like(pre)

    @pl.when(z == 0)
    def _():
        rrecv[...] = jnp.zeros_like(rrecv)

    @pl.when(z == last)
    def _():
        lrecv[...] = jnp.zeros_like(lrecv)

    for h in range(CHUNKS):
        ctx_copy(h).wait()
    res_copy.wait()

    mine = pl.ds(pl.multiple_of(z * rb, rb), rb)
    far = jnp.maximum(z, last - z)

    def lead(c):
        @pl.when(z == 0)
        def _():
            rsend[c] = part[c].astype(BF16)
            rcopy(c).start()

        @pl.when(z == last)
        def _():
            lsend[c] = part[c].astype(BF16)
            lcopy(c).start()

    for j in range(TILES):
        wo_copy(j).wait()
        for q in range(2):
            wi_copy(j, q).start()
        acc = scales[0] * jnp.dot(ctxv[...].reshape(CHUNKS * rows, -1), wov[j], preferred_element_type=F32)
        for h in range(CHUNKS):
            c = h * TILES + j
            part[c] = acc[h * rows:(h + 1) * rows]
            part[c, mine] = part[c, mine] + residv[h * rb:(h + 1) * rb, j * dj:(j + 1) * dj].astype(F32)
        if j == 0:
            pl.semaphore_wait(barrier, jnp.where((z > 0) & (z < last), 4, 3))
        lead(j)

    def leads(c, carry):
        lead(c)
        return carry

    lax.fori_loop(TILES, n, leads, 0)

    def cross(h):
        pcopy(h).wait_recv()
        total = pre[h, p] + precv[h].astype(F32)
        pre[h, p] = total
        xsend[h] = total.astype(BF16)
        for i in range(SUBS):
            xcopy(h, i).start()

    def activate(h, i):
        xcopy(h, i).wait_recv()
        v = pre[h, p, piece(i)] + xrecv[h, piece(i)].astype(F32)
        hid[h, p, piece(i)] = gelu(scales[1] * v).astype(BF16)
        hcopy(h, i, p).start()

    def down(h, j):
        @pl.when(j == 0)
        def _():
            for i in range(SUBS):
                hcopy(h, i, 1 - p).wait_recv()

        @pl.when(h == 0)
        def _():
            wd_copy(j).wait()

        total = jnp.dot(hid[h, 0], wdv[j, :hq], preferred_element_type=F32)
        total += jnp.dot(hid[h, 1], wdv[j, hq:], preferred_element_type=F32)
        total = total.reshape(nb, rb, dj)
        macc[h, j] = total
        mpart[h, j] = total.astype(BF16)
        for d in range(1, nb):
            mcopy(h, j, d).start()

    def step(s, carry):
        cr, cl, cm = s - SKEW * (z - 1), s - SKEW * (last - z - 1), s - SKEW * (far - 1)

        @pl.when(s < TILES)
        def _():
            wd_copy(s).start()

        right = (cr >= 0) & (cr < n) & (z > 0)
        left = (cl >= 0) & (cl < n) & (z < last)

        @pl.when(right)
        def _():
            rcopy(cr).wait_recv()

            @pl.when(z < last)
            def _():
                rsend[cr] = (part[cr] + rrecv[cr].astype(F32)).astype(BF16)
                rcopy(cr).start()

        @pl.when(left)
        def _():
            lcopy(cl).wait_recv()

            @pl.when(z > 0)
            def _():
                lsend[cl] = (part[cl] + lrecv[cl].astype(F32)).astype(BF16)
                lcopy(cl).start()

        @pl.when((cm >= TILES) & (cm <= n) & (lax.rem(jnp.maximum(cm, 0), TILES) == 0))
        def _():
            cross(cm // TILES - 1)

        @pl.when((cm >= 0) & (cm < n))
        def _():
            h, j = cm // TILES, lax.rem(cm, TILES)
            mixed[cm] = (part[cm] + rrecv[cm].astype(F32) + lrecv[cm].astype(F32)).astype(BF16)

            @pl.when(cm < TILES)
            def _():
                for q in range(2):
                    wi_copy(j, q).wait()

            pre[h, 1 - p] += jnp.dot(mixed[cm], wiv[j, 1 - p], preferred_element_type=F32)

            @pl.when(j == TILES - 1)
            def _():
                psend[h] = pre[h, 1 - p].astype(BF16)
                pcopy(h).start()

            pre[h, p] += jnp.dot(mixed[cm], wiv[j, p], preferred_element_type=F32)

        for i in range(SUBS):
            ca = jnp.maximum(cm - TILES - ACT - GAP * i, -1)

            @pl.when((ca >= 0) & (ca < n) & (lax.rem(jnp.maximum(ca, 0), TILES) == 0))
            def _():
                activate(ca // TILES, i)

        cd = jnp.maximum(cm - TILES - DOWN, -1)

        @pl.when((cd >= 0) & (cd < n))
        def _():
            down(cd // TILES, lax.rem(cd, TILES))

        return carry

    lax.fori_loop(0, n + SKEW * (last - 1) + TILES + DOWN, step, 0)

    def out_copy(h):
        return pltpu.make_async_copy(outv.at[h], out.at[pl.ds(h * rb, rb)], out_sem.at[h])

    def finish(h):
        for j in range(TILES):
            total = macc[h, j, z]
            for d in range(1, nb):
                mcopy(h, j, d).wait_recv()
                total += mrecv[h, j, d - 1].astype(F32)
            base = mixed[h * TILES + j, mine].astype(F32)
            outv[h, :, j * dj:(j + 1) * dj] = (base + scales[2] * total).astype(BF16)
        out_copy(h).start()

    def sent(h):
        for j in range(TILES):
            for d in range(1, nb):
                mcopy(h, j, d).wait_send()

    @pl.when(z < last)
    def _():
        for c in range(n):
            rcopy(c).wait_send()

    @pl.when(z > 0)
    def _():
        for c in range(n):
            lcopy(c).wait_send()

    for h in range(CHUNKS):
        pcopy(h).wait_send()
        for i in range(SUBS):
            xcopy(h, i).wait_send()
            hcopy(h, i, p).wait_send()

    for h in range(CHUNKS - 1):
        finish(h)
        sent(h)
    finish(CHUNKS - 1)
    sent(CHUNKS - 1)
    for h in range(CHUNKS):
        out_copy(h).wait()


def fused(nb, resid, context, w_out, w_in, w_down, scales):
    tb, d = resid.shape
    t, k = context.shape
    hidden = w_in.shape[1]
    rows, dj, hq, rb = t // CHUNKS, d // TILES, hidden // 2, tb // CHUNKS
    n, last = CHUNKS * TILES, nb - 1
    any_spec = pl.BlockSpec(memory_space=pl.ANY)
    dma = pltpu.SemaphoreType.DMA
    return pl.pallas_call(
        functools.partial(kernel, nb),
        out_shape=jax.ShapeDtypeStruct((tb, d), BF16),
        in_specs=[pl.BlockSpec(memory_space=pltpu.SMEM)] + [any_spec] * 5,
        out_specs=any_spec,
        scratch_shapes=[
            pltpu.VMEM((CHUNKS, rb, d), BF16),
            pltpu.VMEM((CHUNKS, nb, rb, k), BF16),
            pltpu.VMEM((tb, d), BF16),
            pltpu.VMEM((TILES, k, dj), BF16),
            pltpu.VMEM((TILES, 2, dj, hq), BF16),
            pltpu.VMEM((TILES, hidden, dj), BF16),
            pltpu.VMEM((n, rows, dj), F32),
            pltpu.VMEM((n, rows, dj), BF16),
            pltpu.VMEM((n, rows, dj), BF16),
            pltpu.VMEM((n, rows, dj), BF16),
            pltpu.VMEM((n, rows, dj), BF16),
            pltpu.VMEM((n, rows, dj), BF16),
            pltpu.VMEM((CHUNKS, 2, rows, hq), F32),
            pltpu.VMEM((CHUNKS, rows, hq), BF16),
            pltpu.VMEM((CHUNKS, rows, hq), BF16),
            pltpu.VMEM((CHUNKS, rows, hq), BF16),
            pltpu.VMEM((CHUNKS, rows, hq), BF16),
            pltpu.VMEM((CHUNKS, 2, rows, hq), BF16),
            pltpu.VMEM((CHUNKS, TILES, nb, rb, dj), F32),
            pltpu.VMEM((CHUNKS, TILES, nb, rb, dj), BF16),
            pltpu.VMEM((CHUNKS, TILES, last, rb, dj), BF16),
            dma((CHUNKS,)), dma((CHUNKS,)), dma, dma((TILES,)), dma((TILES * 2,)), dma((TILES,)),
            dma((n,)), dma((n,)), dma((n,)), dma((n,)),
            dma((CHUNKS,)), dma((CHUNKS,)),
            dma((CHUNKS * SUBS,)), dma((CHUNKS * SUBS,)),
            dma((CHUNKS * SUBS,)), dma((CHUNKS * SUBS,)),
            dma((n * last,)), dma((n * last,)),
        ],
        compiler_params=pltpu.CompilerParams(
            collective_id=0, has_side_effects=True, vmem_limit_bytes=67043328
        ),
    )(scales, resid, context.reshape(nb, CHUNKS, rb, k), w_out, w_in, w_down)


def solution(mesh):
    in_specs = (
        P(("groups", "blk"), ("sub", "pair")),
        P("groups", "blk"),
        P("blk", ("sub", "pair")),
        P(("sub", "pair"), "blk"),
        P("blk", ("sub", "pair")),
        P(),
    )
    out_specs = P(("groups", "blk"), ("sub", "pair"))
    nb = mesh.shape["blk"]
    if mesh.shape["sub"] == 2 and mesh.shape["pair"] == 2 and nb > 1:
        body = functools.partial(fused, nb)
    else:
        body = local
    return jax.shard_map(body, mesh=mesh, in_specs=in_specs, out_specs=out_specs, check_vma=False)
```

```python
import functools

import jax
import jax.numpy as jnp
from jax import lax
from jax.experimental import pallas as pl
from jax.experimental.pallas import tpu as pltpu
from jax.sharding import PartitionSpec as P

F32 = jnp.float32
BF16 = jnp.bfloat16
MESH = pl.DeviceIdType.MESH
CHUNKS = 4
TILES = 4
SUBS = 1
ACT = 7
GAP = 2
SKEW = 3
DOWN = 8


def local(resid, context, w_out, w_in, w_down, scales):
    picked = context
    attn = lax.psum_scatter(
        jnp.dot(picked, w_out, preferred_element_type=jnp.float32).astype(jnp.bfloat16),
        "blk",
        scatter_dimension=0,
        tiled=True,
    ).astype(jnp.float32)
    mixed = (resid.astype(jnp.float32) + scales[0] * attn).astype(jnp.bfloat16)
    pre_terms = jnp.dot(
        lax.all_gather(mixed, "blk", axis=0, tiled=True), w_in, preferred_element_type=jnp.float32
    )
    pre_part = lax.psum_scatter(
        pre_terms.astype(jnp.bfloat16), ("sub", "pair"), scatter_dimension=0, tiled=True
    ).astype(jnp.float32)
    hidden_part = jax.nn.gelu(scales[1] * pre_part, approximate=False).astype(jnp.bfloat16)
    hidden = lax.all_gather(hidden_part, ("sub", "pair"), axis=0, tiled=True)
    picked = hidden
    mlp = lax.psum_scatter(
        jnp.dot(picked, w_down, preferred_element_type=jnp.float32).astype(jnp.bfloat16),
        "blk",
        scatter_dimension=0,
        tiled=True,
    ).astype(jnp.float32)
    return (mixed.astype(jnp.float32) + scales[2] * mlp).astype(jnp.bfloat16)


def gelu(v):
    return v * (1.0 + lax.erf(v * (0.5**0.5))) * 0.5


def kernel(
    nb, scales, resid, ctx, wo, wi, wd, out,
    outv, ctxv, residv, wov, wiv, wdv, part, rsend, rrecv, lsend, lrecv, mixed, pre,
    psend, precv, xsend, xrecv, hid, macc, mpart, mrecv,
    out_sem, ctx_sem, res_sem, wo_sem, wi_sem, wd_sem,
    rss, rrs, lss, lrs, pss, prs, xss, xrs, hss, hrs, mss, mrs,
):
    z, x, p = lax.axis_index("blk"), lax.axis_index("sub"), lax.axis_index("pair")
    last = nb - 1
    tb = residv.shape[0]
    rb = tb // CHUNKS
    rows = rb * nb
    dj = wov.shape[2]
    hq = pre.shape[3]
    rs = rows // SUBS
    n = CHUNKS * TILES

    def ctx_copy(h):
        return pltpu.make_async_copy(ctx.at[:, h], ctxv.at[h], ctx_sem.at[h])

    def wo_copy(j):
        return pltpu.make_async_copy(wo.at[:, pl.ds(j * dj, dj)], wov.at[j], wo_sem.at[j])

    def wi_copy(j, q):
        return pltpu.make_async_copy(
            wi.at[pl.ds(j * dj, dj), pl.ds(q * hq, hq)], wiv.at[j, q], wi_sem.at[j * 2 + q]
        )

    def wd_copy(j):
        return pltpu.make_async_copy(wd.at[:, pl.ds(pl.multiple_of(j * dj, dj), dj)], wdv.at[j], wd_sem.at[j])

    res_copy = pltpu.make_async_copy(resid, residv, res_sem)

    def remote(src, dst, ss, rsm, dev):
        return pltpu.make_async_remote_copy(
            src_ref=src, dst_ref=dst, send_sem=ss, recv_sem=rsm, device_id=dev, device_id_type=MESH
        )

    def rcopy(c):
        return remote(rsend.at[c], rrecv.at[c], rss.at[c], rrs.at[c], {"blk": lax.rem(z + 1, nb)})

    def lcopy(c):
        return remote(lsend.at[c], lrecv.at[c], lss.at[c], lrs.at[c], {"blk": lax.rem(z + last, nb)})

    def pcopy(h):
        return remote(psend.at[h], precv.at[h], pss.at[h], prs.at[h], {"pair": 1 - p})

    def piece(i):
        return pl.ds(pl.multiple_of(i * rs, rs), rs)

    def xcopy(h, i):
        return remote(
            xsend.at[h, piece(i)], xrecv.at[h, piece(i)], xss.at[h * SUBS + i], xrs.at[h * SUBS + i], {"sub": 1 - x}
        )

    def hcopy(h, i, q):
        return remote(
            hid.at[h, q, piece(i)], hid.at[h, q, piece(i)], hss.at[h * SUBS + i], hrs.at[h * SUBS + i], {"pair": 1 - p}
        )

    def mcopy(h, j, d):
        to = lax.rem(z + d, nb)
        k = (h * TILES + j) * last + d - 1
        return remote(mpart.at[h, j, to], mrecv.at[h, j, d - 1], mss.at[k], mrs.at[k], {"blk": to})

    barrier = pltpu.get_barrier_semaphore()
    for d in (1, -1):
        @pl.when((z + d >= 0) & (z + d < nb))
        def _():
            pl.semaphore_signal(barrier, inc=1, device_id={"blk": z + d}, device_id_type=MESH)
    pl.semaphore_signal(barrier, inc=1, device_id={"sub": 1 - x}, device_id_type=MESH)
    pl.semaphore_signal(barrier, inc=1, device_id={"pair": 1 - p}, device_id_type=MESH)

    wo_copy(0).start()
    for h in range(CHUNKS):
        ctx_copy(h).start()
    for j in range(1, TILES):
        wo_copy(j).start()
    res_copy.start()

    pre[...] = jnp.zeros_like(pre)

    @pl.when(z == 0)
    def _():
        rrecv[...] = jnp.zeros_like(rrecv)

    @pl.when(z == last)
    def _():
        lrecv[...] = jnp.zeros_like(lrecv)

    for h in range(CHUNKS):
        ctx_copy(h).wait()
    res_copy.wait()

    mine = pl.ds(pl.multiple_of(z * rb, rb), rb)
    far = jnp.maximum(z, last - z)

    def lead(c):
        @pl.when(z == 0)
        def _():
            rsend[c] = part[c].astype(BF16)
            rcopy(c).start()

        @pl.when(z == last)
        def _():
            lsend[c] = part[c].astype(BF16)
            lcopy(c).start()

    for j in range(TILES):
        wo_copy(j).wait()
        for q in range(2):
            wi_copy(j, q).start()
        acc = scales[0] * jnp.dot(ctxv[...].reshape(CHUNKS * rows, -1), wov[j], preferred_element_type=F32)
        for h in range(CHUNKS):
            c = h * TILES + j
            part[c] = acc[h * rows:(h + 1) * rows]
            part[c, mine] = part[c, mine] + residv[h * rb:(h + 1) * rb, j * dj:(j + 1) * dj].astype(F32)
        if j == 0:
            pl.semaphore_wait(barrier, jnp.where((z > 0) & (z < last), 4, 3))
        lead(j)

    def leads(c, carry):
        lead(c)
        return carry

    lax.fori_loop(TILES, n, leads, 0)

    def cross(h):
        pcopy(h).wait_recv()
        total = pre[h, p] + precv[h].astype(F32)
        pre[h, p] = total
        xsend[h] = total.astype(BF16)
        for i in range(SUBS):
            xcopy(h, i).start()

    def activate(h, i):
        xcopy(h, i).wait_recv()
        v = pre[h, p, piece(i)] + xrecv[h, piece(i)].astype(F32)
        hid[h, p, piece(i)] = gelu(scales[1] * v).astype(BF16)
        hcopy(h, i, p).start()

    def down(h, j):
        @pl.when(j == 0)
        def _():
            for i in range(SUBS):
                hcopy(h, i, 1 - p).wait_recv()

        @pl.when(h == 0)
        def _():
            wd_copy(j).wait()

        total = jnp.dot(hid[h, 0], wdv[j, :hq], preferred_element_type=F32)
        total += jnp.dot(hid[h, 1], wdv[j, hq:], preferred_element_type=F32)
        total = total.reshape(nb, rb, dj)
        macc[h, j] = total
        mpart[h, j] = total.astype(BF16)
        for d in range(1, nb):
            mcopy(h, j, d).start()

    def step(s, carry):
        cr, cl, cm = s - SKEW * (z - 1), s - SKEW * (last - z - 1), s - SKEW * (far - 1)

        @pl.when(s < TILES)
        def _():
            wd_copy(s).start()

        right = (cr >= 0) & (cr < n) & (z > 0)
        left = (cl >= 0) & (cl < n) & (z < last)

        @pl.when(right)
        def _():
            rcopy(cr).wait_recv()

            @pl.when(z < last)
            def _():
                rsend[cr] = (part[cr] + rrecv[cr].astype(F32)).astype(BF16)
                rcopy(cr).start()

        @pl.when(left)
        def _():
            lcopy(cl).wait_recv()

            @pl.when(z > 0)
            def _():
                lsend[cl] = (part[cl] + lrecv[cl].astype(F32)).astype(BF16)
                lcopy(cl).start()

        @pl.when((cm >= TILES) & (cm <= n) & (lax.rem(jnp.maximum(cm, 0), TILES) == 0))
        def _():
            cross(cm // TILES - 1)

        @pl.when((cm >= 0) & (cm < n))
        def _():
            h, j = cm // TILES, lax.rem(cm, TILES)
            mixed[cm] = (part[cm] + rrecv[cm].astype(F32) + lrecv[cm].astype(F32)).astype(BF16)

            @pl.when(cm < TILES)
            def _():
                for q in range(2):
                    wi_copy(j, q).wait()

            pre[h, 1 - p] += jnp.dot(mixed[cm], wiv[j, 1 - p], preferred_element_type=F32)

            @pl.when(j == TILES - 1)
            def _():
                psend[h] = pre[h, 1 - p].astype(BF16)
                pcopy(h).start()

            pre[h, p] += jnp.dot(mixed[cm], wiv[j, p], preferred_element_type=F32)

        for i in range(SUBS):
            ca = jnp.maximum(cm - TILES - ACT - GAP * i, -1)

            @pl.when((ca >= 0) & (ca < n) & (lax.rem(jnp.maximum(ca, 0), TILES) == 0))
            def _():
                activate(ca // TILES, i)

        cd = jnp.maximum(cm - TILES - DOWN, -1)

        @pl.when((cd >= 0) & (cd < n))
        def _():
            down(cd // TILES, lax.rem(cd, TILES))

        return carry

    lax.fori_loop(0, n + SKEW * (last - 1) + TILES + DOWN, step, 0)

    def out_copy(h):
        return pltpu.make_async_copy(outv.at[h], out.at[pl.ds(h * rb, rb)], out_sem.at[h])

    def finish(h):
        for j in range(TILES):
            total = macc[h, j, z]
            for d in range(1, nb):
                mcopy(h, j, d).wait_recv()
                total += mrecv[h, j, d - 1].astype(F32)
            base = mixed[h * TILES + j, mine].astype(F32)
            outv[h, :, j * dj:(j + 1) * dj] = (base + scales[2] * total).astype(BF16)
        out_copy(h).start()

    def sent(h):
        for j in range(TILES):
            for d in range(1, nb):
                mcopy(h, j, d).wait_send()

    @pl.when(z < last)
    def _():
        for c in range(n):
            rcopy(c).wait_send()

    @pl.when(z > 0)
    def _():
        for c in range(n):
            lcopy(c).wait_send()

    for h in range(CHUNKS):
        pcopy(h).wait_send()
        for i in range(SUBS):
            xcopy(h, i).wait_send()
            hcopy(h, i, p).wait_send()

    for h in range(CHUNKS - 1):
        finish(h)
        sent(h)
    finish(CHUNKS - 1)
    sent(CHUNKS - 1)
    for h in range(CHUNKS):
        out_copy(h).wait()


def fused(nb, resid, context, w_out, w_in, w_down, scales):
    tb, d = resid.shape
    t, k = context.shape
    hidden = w_in.shape[1]
    rows, dj, hq, rb = t // CHUNKS, d // TILES, hidden // 2, tb // CHUNKS
    n, last = CHUNKS * TILES, nb - 1
    any_spec = pl.BlockSpec(memory_space=pl.ANY)
    dma = pltpu.SemaphoreType.DMA
    return pl.pallas_call(
        functools.partial(kernel, nb),
        out_shape=jax.ShapeDtypeStruct((tb, d), BF16),
        in_specs=[pl.BlockSpec(memory_space=pltpu.SMEM)] + [any_spec] * 5,
        out_specs=any_spec,
        scratch_shapes=[
            pltpu.VMEM((CHUNKS, rb, d), BF16),
            pltpu.VMEM((CHUNKS, nb, rb, k), BF16),
            pltpu.VMEM((tb, d), BF16),
            pltpu.VMEM((TILES, k, dj), BF16),
            pltpu.VMEM((TILES, 2, dj, hq), BF16),
            pltpu.VMEM((TILES, hidden, dj), BF16),
            pltpu.VMEM((n, rows, dj), F32),
            pltpu.VMEM((n, rows, dj), BF16),
            pltpu.VMEM((n, rows, dj), BF16),
            pltpu.VMEM((n, rows, dj), BF16),
            pltpu.VMEM((n, rows, dj), BF16),
            pltpu.VMEM((n, rows, dj), BF16),
            pltpu.VMEM((CHUNKS, 2, rows, hq), F32),
            pltpu.VMEM((CHUNKS, rows, hq), BF16),
            pltpu.VMEM((CHUNKS, rows, hq), BF16),
            pltpu.VMEM((CHUNKS, rows, hq), BF16),
            pltpu.VMEM((CHUNKS, rows, hq), BF16),
            pltpu.VMEM((CHUNKS, 2, rows, hq), BF16),
            pltpu.VMEM((CHUNKS, TILES, nb, rb, dj), F32),
            pltpu.VMEM((CHUNKS, TILES, nb, rb, dj), BF16),
            pltpu.VMEM((CHUNKS, TILES, last, rb, dj), BF16),
            dma((CHUNKS,)), dma((CHUNKS,)), dma, dma((TILES,)), dma((TILES * 2,)), dma((TILES,)),
            dma((n,)), dma((n,)), dma((n,)), dma((n,)),
            dma((CHUNKS,)), dma((CHUNKS,)),
            dma((CHUNKS * SUBS,)), dma((CHUNKS * SUBS,)),
            dma((CHUNKS * SUBS,)), dma((CHUNKS * SUBS,)),
            dma((n * last,)), dma((n * last,)),
        ],
        compiler_params=pltpu.CompilerParams(
            collective_id=0, has_side_effects=True, vmem_limit_bytes=67043328
        ),
    )(scales, resid, context.reshape(nb, CHUNKS, rb, k), w_out, w_in, w_down)


def solution(mesh):
    in_specs = (
        P(("groups", "blk"), ("sub", "pair")),
        P("groups", "blk"),
        P("blk", ("sub", "pair")),
        P(("sub", "pair"), "blk"),
        P("blk", ("sub", "pair")),
        P(),
    )
    out_specs = P(("groups", "blk"), ("sub", "pair"))
    nb = mesh.shape["blk"]
    if mesh.shape["sub"] == 2 and mesh.shape["pair"] == 2 and nb > 1:
        body = functools.partial(fused, nb)
    else:
        body = local
    return jax.shard_map(body, mesh=mesh, in_specs=in_specs, out_specs=out_specs, check_vma=False)
```

```python
import functools

import jax
import jax.numpy as jnp
from jax import lax
from jax.experimental import pallas as pl
from jax.experimental.pallas import tpu as pltpu
from jax.sharding import PartitionSpec as P

F32 = jnp.float32
BF16 = jnp.bfloat16
MESH = pl.DeviceIdType.MESH
CHUNKS = 4
TILES = 4
SUBS = 1
ACT = 6
GAP = 2
SKEW = 3
DOWN = 7


def local(resid, context, w_out, w_in, w_down, scales):
    picked = context
    attn = lax.psum_scatter(
        jnp.dot(picked, w_out, preferred_element_type=jnp.float32).astype(jnp.bfloat16),
        "blk",
        scatter_dimension=0,
        tiled=True,
    ).astype(jnp.float32)
    mixed = (resid.astype(jnp.float32) + scales[0] * attn).astype(jnp.bfloat16)
    pre_terms = jnp.dot(
        lax.all_gather(mixed, "blk", axis=0, tiled=True), w_in, preferred_element_type=jnp.float32
    )
    pre_part = lax.psum_scatter(
        pre_terms.astype(jnp.bfloat16), ("sub", "pair"), scatter_dimension=0, tiled=True
    ).astype(jnp.float32)
    hidden_part = jax.nn.gelu(scales[1] * pre_part, approximate=False).astype(jnp.bfloat16)
    hidden = lax.all_gather(hidden_part, ("sub", "pair"), axis=0, tiled=True)
    picked = hidden
    mlp = lax.psum_scatter(
        jnp.dot(picked, w_down, preferred_element_type=jnp.float32).astype(jnp.bfloat16),
        "blk",
        scatter_dimension=0,
        tiled=True,
    ).astype(jnp.float32)
    return (mixed.astype(jnp.float32) + scales[2] * mlp).astype(jnp.bfloat16)


def gelu(v):
    return v * (1.0 + lax.erf(v * (0.5**0.5))) * 0.5


def kernel(
    nb, scales, resid, ctx, wo, wi, wd, out,
    outv, ctxv, residv, wov, wiv, wdv, part, rsend, rrecv, lsend, lrecv, mixed, pre,
    psend, precv, xsend, xrecv, hid, macc, mpart, mrecv,
    out_sem, ctx_sem, res_sem, wo_sem, wi_sem, wd_sem,
    rss, rrs, lss, lrs, pss, prs, xss, xrs, hss, hrs, mss, mrs,
):
    z, x, p = lax.axis_index("blk"), lax.axis_index("sub"), lax.axis_index("pair")
    last = nb - 1
    tb = residv.shape[0]
    rb = tb // CHUNKS
    rows = rb * nb
    dj = wov.shape[2]
    hq = pre.shape[3]
    rs = rows // SUBS
    n = CHUNKS * TILES

    def ctx_copy(h):
        return pltpu.make_async_copy(ctx.at[:, h], ctxv.at[h], ctx_sem.at[h])

    def wo_copy(j):
        return pltpu.make_async_copy(wo.at[:, pl.ds(j * dj, dj)], wov.at[j], wo_sem.at[j])

    def wi_copy(j, q):
        return pltpu.make_async_copy(
            wi.at[pl.ds(j * dj, dj), pl.ds(q * hq, hq)], wiv.at[j, q], wi_sem.at[j * 2 + q]
        )

    def wd_copy(j):
        return pltpu.make_async_copy(wd.at[:, pl.ds(pl.multiple_of(j * dj, dj), dj)], wdv.at[j], wd_sem.at[j])

    res_copy = pltpu.make_async_copy(resid, residv, res_sem)

    def remote(src, dst, ss, rsm, dev):
        return pltpu.make_async_remote_copy(
            src_ref=src, dst_ref=dst, send_sem=ss, recv_sem=rsm, device_id=dev, device_id_type=MESH
        )

    def rcopy(c):
        return remote(rsend.at[c], rrecv.at[c], rss.at[c], rrs.at[c], {"blk": lax.rem(z + 1, nb)})

    def lcopy(c):
        return remote(lsend.at[c], lrecv.at[c], lss.at[c], lrs.at[c], {"blk": lax.rem(z + last, nb)})

    def pcopy(h):
        return remote(psend.at[h], precv.at[h], pss.at[h], prs.at[h], {"pair": 1 - p})

    def piece(i):
        return pl.ds(pl.multiple_of(i * rs, rs), rs)

    def xcopy(h, i):
        return remote(
            xsend.at[h, piece(i)], xrecv.at[h, piece(i)], xss.at[h * SUBS + i], xrs.at[h * SUBS + i], {"sub": 1 - x}
        )

    def hcopy(h, i, q):
        return remote(
            hid.at[h, q, piece(i)], hid.at[h, q, piece(i)], hss.at[h * SUBS + i], hrs.at[h * SUBS + i], {"pair": 1 - p}
        )

    def mcopy(h, j, d):
        to = lax.rem(z + d, nb)
        k = (h * TILES + j) * last + d - 1
        return remote(mpart.at[h, j, to], mrecv.at[h, j, d - 1], mss.at[k], mrs.at[k], {"blk": to})

    barrier = pltpu.get_barrier_semaphore()
    for d in (1, -1):
        @pl.when((z + d >= 0) & (z + d < nb))
        def _():
            pl.semaphore_signal(barrier, inc=1, device_id={"blk": z + d}, device_id_type=MESH)
    pl.semaphore_signal(barrier, inc=1, device_id={"sub": 1 - x}, device_id_type=MESH)
    pl.semaphore_signal(barrier, inc=1, device_id={"pair": 1 - p}, device_id_type=MESH)

    wo_copy(0).start()
    for h in range(CHUNKS):
        ctx_copy(h).start()
    for j in range(1, TILES):
        wo_copy(j).start()
    res_copy.start()

    pre[...] = jnp.zeros_like(pre)

    @pl.when(z == 0)
    def _():
        rrecv[...] = jnp.zeros_like(rrecv)

    @pl.when(z == last)
    def _():
        lrecv[...] = jnp.zeros_like(lrecv)

    for h in range(CHUNKS):
        ctx_copy(h).wait()
    res_copy.wait()

    mine = pl.ds(pl.multiple_of(z * rb, rb), rb)
    far = jnp.maximum(z, last - z)

    def lead(c):
        @pl.when(z == 0)
        def _():
            rsend[c] = part[c].astype(BF16)
            rcopy(c).start()

        @pl.when(z == last)
        def _():
            lsend[c] = part[c].astype(BF16)
            lcopy(c).start()

    for j in range(TILES):
        wo_copy(j).wait()
        for q in range(2):
            wi_copy(j, q).start()
        acc = scales[0] * jnp.dot(ctxv[...].reshape(CHUNKS * rows, -1), wov[j], preferred_element_type=F32)
        for h in range(CHUNKS):
            c = h * TILES + j
            part[c] = acc[h * rows:(h + 1) * rows]
            part[c, mine] = part[c, mine] + residv[h * rb:(h + 1) * rb, j * dj:(j + 1) * dj].astype(F32)
        if j == 0:
            pl.semaphore_wait(barrier, jnp.where((z > 0) & (z < last), 4, 3))
        lead(j)

    def leads(c, carry):
        lead(c)
        return carry

    lax.fori_loop(TILES, n, leads, 0)

    def cross(h):
        pcopy(h).wait_recv()
        total = pre[h, p] + precv[h].astype(F32)
        pre[h, p] = total
        xsend[h] = total.astype(BF16)
        for i in range(SUBS):
            xcopy(h, i).start()

    def activate(h, i):
        xcopy(h, i).wait_recv()
        v = pre[h, p, piece(i)] + xrecv[h, piece(i)].astype(F32)
        hid[h, p, piece(i)] = gelu(scales[1] * v).astype(BF16)
        hcopy(h, i, p).start()

    def down(h, j):
        @pl.when(j == 0)
        def _():
            for i in range(SUBS):
                hcopy(h, i, 1 - p).wait_recv()

        @pl.when(h == 0)
        def _():
            wd_copy(j).wait()

        total = jnp.dot(hid[h, 0], wdv[j, :hq], preferred_element_type=F32)
        total += jnp.dot(hid[h, 1], wdv[j, hq:], preferred_element_type=F32)
        total = total.reshape(nb, rb, dj)
        macc[h, j] = total
        mpart[h, j] = total.astype(BF16)
        for d in range(1, nb):
            mcopy(h, j, d).start()

    def step(s, carry):
        cr, cl, cm = s - SKEW * (z - 1), s - SKEW * (last - z - 1), s - SKEW * (far - 1)

        @pl.when(s < TILES)
        def _():
            wd_copy(s).start()

        right = (cr >= 0) & (cr < n) & (z > 0)
        left = (cl >= 0) & (cl < n) & (z < last)

        @pl.when(right)
        def _():
            rcopy(cr).wait_recv()

            @pl.when(z < last)
            def _():
                rsend[cr] = (part[cr] + rrecv[cr].astype(F32)).astype(BF16)
                rcopy(cr).start()

        @pl.when(left)
        def _():
            lcopy(cl).wait_recv()

            @pl.when(z > 0)
            def _():
                lsend[cl] = (part[cl] + lrecv[cl].astype(F32)).astype(BF16)
                lcopy(cl).start()

        @pl.when((cm >= TILES) & (cm <= n) & (lax.rem(jnp.maximum(cm, 0), TILES) == 0))
        def _():
            cross(cm // TILES - 1)

        @pl.when((cm >= 0) & (cm < n))
        def _():
            h, j = cm // TILES, lax.rem(cm, TILES)
            mixed[cm] = (part[cm] + rrecv[cm].astype(F32) + lrecv[cm].astype(F32)).astype(BF16)

            @pl.when(cm < TILES)
            def _():
                for q in range(2):
                    wi_copy(j, q).wait()

            pre[h, 1 - p] += jnp.dot(mixed[cm], wiv[j, 1 - p], preferred_element_type=F32)

            @pl.when(j == TILES - 1)
            def _():
                psend[h] = pre[h, 1 - p].astype(BF16)
                pcopy(h).start()

            pre[h, p] += jnp.dot(mixed[cm], wiv[j, p], preferred_element_type=F32)

        for i in range(SUBS):
            ca = jnp.maximum(cm - TILES - ACT - GAP * i, -1)

            @pl.when((ca >= 0) & (ca < n) & (lax.rem(jnp.maximum(ca, 0), TILES) == 0))
            def _():
                activate(ca // TILES, i)

        cd = jnp.maximum(cm - TILES - DOWN, -1)

        @pl.when((cd >= 0) & (cd < n))
        def _():
            down(cd // TILES, lax.rem(cd, TILES))

        return carry

    lax.fori_loop(0, n + SKEW * (last - 1) + TILES + DOWN, step, 0)

    def out_copy(h):
        return pltpu.make_async_copy(outv.at[h], out.at[pl.ds(h * rb, rb)], out_sem.at[h])

    def finish(h):
        for j in range(TILES):
            total = macc[h, j, z]
            for d in range(1, nb):
                mcopy(h, j, d).wait_recv()
                total += mrecv[h, j, d - 1].astype(F32)
            base = mixed[h * TILES + j, mine].astype(F32)
            outv[h, :, j * dj:(j + 1) * dj] = (base + scales[2] * total).astype(BF16)
        out_copy(h).start()

    def sent(h):
        for j in range(TILES):
            for d in range(1, nb):
                mcopy(h, j, d).wait_send()

    @pl.when(z < last)
    def _():
        for c in range(n):
            rcopy(c).wait_send()

    @pl.when(z > 0)
    def _():
        for c in range(n):
            lcopy(c).wait_send()

    for h in range(CHUNKS):
        pcopy(h).wait_send()
        for i in range(SUBS):
            xcopy(h, i).wait_send()
            hcopy(h, i, p).wait_send()

    for h in range(CHUNKS - 1):
        finish(h)
        sent(h)
    finish(CHUNKS - 1)
    sent(CHUNKS - 1)
    for h in range(CHUNKS):
        out_copy(h).wait()


def fused(nb, resid, context, w_out, w_in, w_down, scales):
    tb, d = resid.shape
    t, k = context.shape
    hidden = w_in.shape[1]
    rows, dj, hq, rb = t // CHUNKS, d // TILES, hidden // 2, tb // CHUNKS
    n, last = CHUNKS * TILES, nb - 1
    any_spec = pl.BlockSpec(memory_space=pl.ANY)
    dma = pltpu.SemaphoreType.DMA
    return pl.pallas_call(
        functools.partial(kernel, nb),
        out_shape=jax.ShapeDtypeStruct((tb, d), BF16),
        in_specs=[pl.BlockSpec(memory_space=pltpu.SMEM)] + [any_spec] * 5,
        out_specs=any_spec,
        scratch_shapes=[
            pltpu.VMEM((CHUNKS, rb, d), BF16),
            pltpu.VMEM((CHUNKS, nb, rb, k), BF16),
            pltpu.VMEM((tb, d), BF16),
            pltpu.VMEM((TILES, k, dj), BF16),
            pltpu.VMEM((TILES, 2, dj, hq), BF16),
            pltpu.VMEM((TILES, hidden, dj), BF16),
            pltpu.VMEM((n, rows, dj), F32),
            pltpu.VMEM((n, rows, dj), BF16),
            pltpu.VMEM((n, rows, dj), BF16),
            pltpu.VMEM((n, rows, dj), BF16),
            pltpu.VMEM((n, rows, dj), BF16),
            pltpu.VMEM((n, rows, dj), BF16),
            pltpu.VMEM((CHUNKS, 2, rows, hq), F32),
            pltpu.VMEM((CHUNKS, rows, hq), BF16),
            pltpu.VMEM((CHUNKS, rows, hq), BF16),
            pltpu.VMEM((CHUNKS, rows, hq), BF16),
            pltpu.VMEM((CHUNKS, rows, hq), BF16),
            pltpu.VMEM((CHUNKS, 2, rows, hq), BF16),
            pltpu.VMEM((CHUNKS, TILES, nb, rb, dj), F32),
            pltpu.VMEM((CHUNKS, TILES, nb, rb, dj), BF16),
            pltpu.VMEM((CHUNKS, TILES, last, rb, dj), BF16),
            dma((CHUNKS,)), dma((CHUNKS,)), dma, dma((TILES,)), dma((TILES * 2,)), dma((TILES,)),
            dma((n,)), dma((n,)), dma((n,)), dma((n,)),
            dma((CHUNKS,)), dma((CHUNKS,)),
            dma((CHUNKS * SUBS,)), dma((CHUNKS * SUBS,)),
            dma((CHUNKS * SUBS,)), dma((CHUNKS * SUBS,)),
            dma((n * last,)), dma((n * last,)),
        ],
        compiler_params=pltpu.CompilerParams(
            collective_id=0, has_side_effects=True, vmem_limit_bytes=67043328
        ),
    )(scales, resid, context.reshape(nb, CHUNKS, rb, k), w_out, w_in, w_down)


def solution(mesh):
    in_specs = (
        P(("groups", "blk"), ("sub", "pair")),
        P("groups", "blk"),
        P("blk", ("sub", "pair")),
        P(("sub", "pair"), "blk"),
        P("blk", ("sub", "pair")),
        P(),
    )
    out_specs = P(("groups", "blk"), ("sub", "pair"))
    nb = mesh.shape["blk"]
    if mesh.shape["sub"] == 2 and mesh.shape["pair"] == 2 and nb > 1:
        body = functools.partial(fused, nb)
    else:
        body = local
    return jax.shard_map(body, mesh=mesh, in_specs=in_specs, out_specs=out_specs, check_vma=False)
```
